256 devices in a mesh: leaf: 32 (over x, y, core), rhs: 8 (over z).
Axes of the slice: x: 4, y: 4, z: 8, core: 2. Of those that a mesh axis runs over, the one named last changes fastest.
Arguments:
- charges: bfloat16 [262144, 4096], P(('leaf', 'rhs')), may hold values from -6 to 6
- leaf_coef: bfloat16 [512, 256, 512], P(('leaf', 'rhs')), may hold values from -0.25 to 0.25
- leaf_rows: int32 [512, 256], P(('leaf', 'rhs')), may hold values from 0 to 511, as said below
- local_interp: bfloat16 [480, 256, 512], P('leaf'), may hold values from -0.25 to 0.25
- top_interp: bfloat16 [7936, 512], P('leaf'), may hold values from -0.25 to 0.25
Outputs:
- subtree_skel: bfloat16 [8192, 4096], P('leaf', 'rhs')
- top_skel: bfloat16 [7936, 4096], P('leaf', 'rhs')
The draws below stay inside these ranges and needn't reach their ends.
Inputs may be any that keep to these rules, and one draw needn't show every extreme that they name: `leaf_rows`: each row holds 256 distinct positions.
All inputs are finite; a program needn't handle non-finite values.
Results may differ from the reference program's by a relative error of at most 0.012.
Values may be sent and summed in bfloat16 or wider, within the bound.
No kernel may reach another device: no remote copies, remote signals or barrier semaphores. Data moves between devices by JAX's collectives and lax.ppermute only.
A program may use at most 64 MiB of HBM per device.

```python
import jax
import jax.numpy as jnp
from jax import lax

S = 256
M = 512
LEAVES_DEV = 16
LEAVES = 512
COLS = 4096
PACK = 248
N_LEAF = 32


def draw_leaf_rows(key, part):
    scores = jax.random.randint(key, (LEAVES, M), 0, 1 << 20) * M + jnp.arange(M, dtype=jnp.int32)[None, :]
    order = jnp.argsort(scores, axis=1, stable=True)
    return order[:, :S].astype(jnp.int32)


def steps_of(own_key, dims, cuts, low, high):
    gain, own = 1.0, jax.random.fold_in(own_key, 6)
    for axis_at, parts in cuts:
        steps = jnp.exp(jax.random.uniform(jax.random.fold_in(own, axis_at), (parts,), jnp.float32, low / len(cuts), high / len(cuts)))
        gain = gain * jnp.repeat(steps, dims[axis_at] // parts).reshape([-1 if axis == axis_at else 1 for axis in range(len(dims))])
    return gain


def scatter_about(own_key, shape, scale, limit, cuts=(), kind=jnp.bfloat16):
    entries = jax.random.normal(own_key, shape, jnp.float32) * scale
    if len(cuts) > 0:
        entries = steps_of(own_key, shape, cuts, -0.22, 0.18) * entries
    return jnp.clip(entries, min=-limit, max=limit).astype(kind)


def setup_inputs(seed: int = 0) -> dict:
    arg_keys = jax.random.split(jax.random.key(seed), 6)
    return {
        "charges": scatter_about(arg_keys[0], (LEAVES * M, COLS), 1.0, 6.0, ((0, 256),)),
        "leaf_coef": scatter_about(arg_keys[1], (LEAVES, S, M), M ** -0.5, 0.25, ((0, 256),)),
        "leaf_rows": draw_leaf_rows(jax.random.fold_in(arg_keys[5], 71), 0),
        "local_interp": scatter_about(arg_keys[3], (N_LEAF * (LEAVES_DEV - 1), S, 2 * S), (2 * S) ** -0.5, 0.25, ((0, 32),)),
        "top_interp": scatter_about(arg_keys[4], (N_LEAF * PACK, 2 * S), (2 * S) ** -0.5, 0.25, ((0, 32),)),
    }


def pick_rows(block, chosen):
    return block[chosen]


def subtree(operand):
    points, coef, chosen, interp = operand
    picked = jax.vmap(pick_rows)(points, chosen).astype(jnp.float32)
    mixed = jnp.einsum("nsm,nmc->nsc", coef.astype(jnp.float32), points.astype(jnp.float32))
    skeleton = (picked + mixed).astype(jnp.bfloat16)
    offset = 0
    node_count = LEAVES_DEV
    while node_count > 1:
        node_count = node_count // 2
        stacked = skeleton.reshape(node_count, 2 * S, COLS)
        matrices = interp[offset:offset + node_count]
        skeleton = jnp.einsum("nij,njc->nic", matrices.astype(jnp.float32), stacked.astype(jnp.float32)).astype(jnp.bfloat16)
        offset = offset + node_count
    return skeleton[0]


def reference(charges, leaf_coef, leaf_rows, local_interp, top_interp):
    points = charges.reshape(N_LEAF, LEAVES_DEV, M, COLS)
    coef = leaf_coef.reshape(N_LEAF, LEAVES_DEV, S, M)
    chosen = leaf_rows.reshape(N_LEAF, LEAVES_DEV, S)
    interp = local_interp.reshape(N_LEAF, LEAVES_DEV - 1, S, 2 * S)
    roots = lax.map(subtree, (points, coef, chosen, interp))
    blocks = top_interp.reshape(N_LEAF, PACK, 2 * S)
    top_levels = N_LEAF.bit_length() - 1
    skeleton = roots
    pieces = []
    for level in range(1, top_levels + 1):
        row_count = S >> level
        offset = S - (S >> (level - 1))
        node_count = N_LEAF >> level
        matrices = blocks[:, offset:offset + row_count].reshape(node_count, S, 2 * S)
        stacked = skeleton.reshape(node_count, 2 * S, COLS)
        skeleton = jnp.einsum("nij,njc->nic", matrices.astype(jnp.float32), stacked.astype(jnp.float32)).astype(jnp.bfloat16)
        pieces.append(skeleton.reshape(N_LEAF, row_count, COLS))
    top_skel = jnp.concatenate(pieces, axis=1).reshape(N_LEAF * PACK, COLS)
    return roots.reshape(N_LEAF * S, COLS), top_skel
```

```python
import functools

import jax
import jax.numpy as jnp
from jax import lax
from jax.experimental import pallas as pl
from jax.experimental.pallas import tpu as pltpu
from jax.sharding import PartitionSpec as P

BF = jnp.bfloat16
F32 = jnp.float32

ORDER = (4, 3, 5, 2, 6, 1, 7, 0)


def mm(a, b):
    return jnp.dot(a, b, preferred_element_type=F32)


def shift(x, distance):
    n = lax.axis_size("rhs")
    return lax.ppermute(x, "rhs", [(i, (i + distance) % n) for i in range(n)])


def swap(x, bits):
    n = lax.axis_size("leaf")
    return lax.ppermute(x, "leaf", [(i, i ^ bits) for i in range(n)])


def add(a, b):
    return (a.astype(F32) + b.astype(F32)).astype(BF)


def leaf_kernel(z_ref, l4, l3, l2, l1, coef, rows, c_ref, out_ref, t_ref):
    @pl.when(pl.program_id(0) == 0)
    def _():
        a = mm(l4[0], l3[0]).astype(BF)
        a = mm(a, l2[0]).astype(BF)
        g = mm(a, l1[0]).astype(BF)
        skel = l1.shape[1]
        size = coef.shape[2]
        for j in range(coef.shape[0]):
            gj = g[:, j * skel : (j + 1) * skel]
            at = lax.broadcasted_iota(jnp.int32, (size, skel), 0)
            pick = jnp.where(at == rows[j : j + 1, :], 1.0, 0.0).astype(BF)
            t = mm(gj, coef[j]) + lax.dot_general(
                gj, pick, (((1,), (1,)), ((), ())), preferred_element_type=F32
            )
            t_ref[:, j * size : (j + 1) * size] = t.astype(BF)

    out_ref[0] = mm(t_ref[...], c_ref[...]).astype(BF)


def leaf_part(z, charges, leaf_coef, leaf_rows, local_interp):
    skel = leaf_coef.shape[1]
    rows_here, cols = charges.shape
    blocks = len(ORDER)
    width = cols // blocks

    def column(i, z_ref):
        rel = jnp.where(i == 7, 0, jnp.where(i % 2 == 1, 3 - i // 2, 4 + i // 2))
        return (z_ref[0] + rel) % blocks

    spec = pltpu.PrefetchScalarGridSpec(
        num_scalar_prefetch=1,
        grid=(blocks,),
        in_specs=[
            pl.BlockSpec((1, skel, skel), lambda i, z: (14, 0, z[0] // 4)),
            pl.BlockSpec((1, skel, skel), lambda i, z: (12 + z[0] // 4, 0, z[0] // 2 % 2)),
            pl.BlockSpec((1, skel, skel), lambda i, z: (8 + z[0] // 2, 0, z[0] % 2)),
            pl.BlockSpec((1, skel, 2 * skel), lambda i, z: (z[0], 0, 0)),
            pl.BlockSpec(leaf_coef.shape, lambda i, z: (0, 0, 0)),
            pl.BlockSpec(leaf_rows.shape, lambda i, z: (0, 0)),
            pl.BlockSpec((rows_here, width), lambda i, z: (0, column(i, z))),
        ],
        out_specs=pl.BlockSpec((1, skel, width), lambda i, z: (i, 0, 0)),
        scratch_shapes=[pltpu.VMEM((skel, rows_here), BF)],
    )
    return pl.pallas_call(
        leaf_kernel,
        grid_spec=spec,
        out_shape=jax.ShapeDtypeStruct((blocks, skel, width), BF),
        name="leaf_part",
    )(z, local_interp, local_interp, local_interp, local_interp, leaf_coef, leaf_rows, charges)


def ring_sum(part):
    s = {rel: part[i] for i, rel in enumerate(ORDER)}
    half = part.shape[1] // 2
    p = shift(s[4][:half], 1)
    m = shift(s[4][half:], -1)
    up = jnp.concatenate([add(s[3][:half], p), s[3][half:]], 0)
    down = jnp.concatenate([s[5][:half], add(s[5][half:], m)], 0)
    for k in (2, 1):
        p = shift(up, 1)
        m = shift(down, -1)
        up = add(s[k], p)
        down = add(s[8 - k], m)
    p = shift(up, 1)
    m = shift(down, -1)
    return (s[0].astype(F32) + p.astype(F32) + m.astype(F32)).astype(BF)


def compose_kernel(pos, w, wp, q_ref, p1_ref, pn):
    x, y, c = pos[0] // 8, pos[0] // 2 % 4, pos[0] % 2
    both = ((w, c), (wp, 1 - c))
    base = (128, 288, 448 - 64, 544 - 64)

    def half(ref, at, count, h):
        return ref[at : at + count, pl.ds(pl.multiple_of(h * 256, 256), 256)]

    def put(at, size, value):
        pn[pl.ds(pl.multiple_of(at * size, size), size), :] = value

    for ref, core in both:
        p1_ref[pl.ds(pl.multiple_of(core * 128, 128), 128), :] = ref[0:128, :]
    h2, h3, h4, h5 = y % 2, y // 2, x % 2, x // 2
    for ref, core in both:
        for ky in (0, 1):
            put((y ^ ky) % 2 * 2 + core, 64, half(ref, base[ky], 64, h2))
    q2 = pn[...]
    for ref, core in both:
        for ky in range(4):
            put((y ^ ky) * 2 + core, 32, half(ref, base[ky] + 64, 32, h3))
    q3 = mm(pn[...], q2).astype(BF)
    for ref, core in both:
        for ky in range(4):
            for kx in (0, 1):
                put((x ^ kx) % 2 * 8 + (y ^ ky) * 2 + core, 16, half(ref, base[ky] + 96 + 16 * kx, 16, h4))
    q4 = mm(pn[...], q3).astype(BF)

    r3 = [mm(half(w, base[ky] + 64, 32, h3), q2) for ky in range(4)]
    r4 = [mm(half(w, base[ky] + 96, 32, h4), q3) for ky in range(4)]
    r5 = [mm(half(w, base[ky] + 128, 32, h5), q4) for ky in range(4)]

    def level4(kx):
        return [r4[ky][16 * kx : 16 * kx + 16] for ky in range(4)]

    def level5(kx):
        return [r5[ky][8 * kx : 8 * kx + 8] for ky in range(4)]

    q_ref[0:160, :] = jnp.concatenate(level4(1) + level5(1) + level5(2) + level5(3), 0).astype(BF)
    q_ref[160:224, :] = half(w, base[0], 64, h2)
    q_ref[224:288, :] = half(w, base[1], 64, h2)
    q_ref[288:512, :] = jnp.concatenate(r3 + level4(0) + level5(0), 0).astype(BF)


def top_kernel(pos, q, p1, own, other, first_ref, s1_ref, s2_ref, s3_ref, keep_ref, node):
    c = pos[0] % 2
    mine = p1[:, pl.ds(pl.multiple_of(c * 256, 256), 256)]
    theirs = p1[:, pl.ds(pl.multiple_of((1 - c) * 256, 256), 256)]
    n1 = (mm(mine, own[...]) + mm(theirs, other[...])).astype(BF)
    node[...] = n1
    first_ref[...] = node[pl.ds(pl.multiple_of(c * 128, 128), 128), :]
    out = mm(q[...], n1).astype(BF)
    s1_ref[...] = out[0:96]
    s2_ref[...] = out[96:128]
    s3_ref[...] = out[128:160]
    keep_ref[...] = out[160:512]


def middle_kernel(keep, a1, a2, a3, own_ref, b1_ref, b2_ref, b3_ref):
    l2 = keep[0:128].astype(F32)
    l3 = keep[128:256].astype(F32)
    l4 = keep[256:320].astype(F32) + a1[0:64].astype(F32)
    l5 = keep[320:352].astype(F32) + a1[64:96].astype(F32) + a2[...].astype(F32) + a3[...].astype(F32)
    for ky, ref in enumerate((own_ref, b1_ref, b2_ref, b3_ref)):
        parts = [l3[32 * ky : 32 * ky + 32], l4[16 * ky : 16 * ky + 16], l5[8 * ky : 8 * ky + 8]]
        if ky < 2:
            parts = [l2[64 * ky : 64 * ky + 64]] + parts
        ref[...] = jnp.concatenate(parts, 0).astype(ref.dtype)


def last_kernel(first, own, b1, b2, b3, out_ref):
    out_ref[0:128, :] = first[...]
    total = own[...] + b1[...].astype(F32)
    out_ref[128:192, :] = total[0:64].astype(BF)
    out_ref[192:248, :] = (total[64:120] + b2[...].astype(F32) + b3[...].astype(F32)).astype(BF)


def whole_call(kernel, shapes, scratch=(), scalars=0, name=None):
    vm = pl.BlockSpec(memory_space=pltpu.VMEM)
    sm = pl.BlockSpec(memory_space=pltpu.SMEM)

    def call(*args):
        return pl.pallas_call(
            kernel,
            in_specs=[sm] * scalars + [vm] * (len(args) - scalars),
            out_specs=[vm] * len(shapes),
            out_shape=[jax.ShapeDtypeStruct(shape, dtype) for shape, dtype in shapes],
            scratch_shapes=list(scratch),
            name=name,
        )(*args)

    return call


def gather_matrices(m):
    x1 = swap(m[224:248], 8)
    x2 = swap(m[240:248], 16)
    x3 = swap(m[240:248], 24)
    v = jnp.concatenate([m[0:240], x1[0:16], m[240:248], x1[16:24], x2, x3], 0)
    y1 = swap(v[128:288], 2)
    y2 = swap(v[192:288], 4)
    y3 = swap(v[192:288], 6)
    w = jnp.concatenate([v, y1, y2, y3], 0)
    return w, swap(w, 1)


def local(charges, leaf_coef, leaf_rows, local_interp, top_interp):
    z = lax.axis_index("rhs").astype(jnp.int32).reshape(1)
    pos = lax.axis_index("leaf").astype(jnp.int32).reshape(1)
    part = leaf_part(z, charges, leaf_coef, leaf_rows, local_interp)
    w, wp = gather_matrices(top_interp)
    q, p1 = whole_call(
        compose_kernel, [((512, 256), BF), ((256, 512), BF)], [pltpu.VMEM((256, 256), BF)], 1, "compose"
    )(pos, w, wp)
    root = ring_sum(part)
    other = swap(root, 1)
    width = root.shape[1]
    first, s1, s2, s3, keep = whole_call(
        top_kernel,
        [((rows, width), BF) for rows in (128, 96, 32, 32, 352)],
        [pltpu.VMEM(root.shape, BF)],
        1,
        "top",
    )(pos, q, p1, root, other)
    a1, a2, a3 = swap(s1, 8), swap(s2, 16), swap(s3, 24)
    own, b1, b2, b3 = whole_call(
        middle_kernel,
        [((120, width), F32), ((120, width), BF), ((56, width), BF), ((56, width), BF)],
        name="middle",
    )(keep, a1, a2, a3)
    b1, b2, b3 = swap(b1, 2), swap(b2, 4), swap(b3, 6)
    (top_skel,) = whole_call(last_kernel, [((248, width), BF)], name="last")(first, own, b1, b2, b3)
    return root, top_skel


def solution(mesh):
    placed = (
        P(("leaf", "rhs"), None),
        P(("leaf", "rhs"), None, None),
        P(("leaf", "rhs"), None),
        P("leaf", None, None),
        P("leaf", None),
    )
    return jax.shard_map(
        local,
        mesh=mesh,
        in_specs=placed,
        out_specs=(P("leaf", "rhs"), P("leaf", "rhs")),
        check_vma=False,
    )
```

```python
import functools

import jax
import jax.numpy as jnp
from jax import lax
from jax.experimental import pallas as pl
from jax.experimental.pallas import tpu as pltpu
from jax.sharding import PartitionSpec as P


BF = jnp.bfloat16
F32 = jnp.float32

ORDER = (4, 3, 5, 2, 6, 1, 7, 0)


def mm(a, b):
    return jnp.dot(a, b, preferred_element_type=F32)


def shift(x, distance):
    leaves, n = lax.axis_size("leaf"), lax.axis_size("rhs")
    pairs = []
    for leaf in range(leaves):
        step = -distance if leaf % 2 else distance
        pairs += [(leaf * n + i, leaf * n + (i + step) % n) for i in range(n)]
    return lax.ppermute(x, ("leaf", "rhs"), pairs)


def column(place, rel, width):
    n = len(ORDER)
    block = (place % n + jnp.where(place < n, rel, n - rel)) % n
    return pl.multiple_of(block * width, width)


def swap(x, bits):
    n = lax.axis_size("leaf")
    return lax.ppermute(x, "leaf", [(i, i ^ bits) for i in range(n)])


def vmem(x):
    return pltpu.with_memory_space_constraint(x, pltpu.VMEM)


def hbm(x):
    return pltpu.with_memory_space_constraint(x, pltpu.HBM)


def paced(x, *after):
    return lax.optimization_barrier((x, *after))[0]


def add(a, b):
    return (a.astype(F32) + b.astype(F32)).astype(BF)


def first_kernel(z_ref, l4, l3, l2, l1, coef, rows, charges, t_ref, out_ref, block, sem):
    width = block.shape[1]
    at = column(z_ref[0], ORDER[0], width)
    copy = pltpu.make_async_copy(charges.at[:, pl.ds(at, width)], block, sem)
    copy.start()
    a = mm(l4[0], l3[0]).astype(BF)
    a = mm(a, l2[0]).astype(BF)
    g = mm(a, l1[0]).astype(BF)
    skel = l1.shape[1]
    size = coef.shape[2]
    for j in range(coef.shape[0]):
        gj = g[:, j * skel : (j + 1) * skel]
        where = lax.broadcasted_iota(jnp.int32, (size, skel), 0)
        pick = jnp.where(where == rows[j : j + 1, :], 1.0, 0.0).astype(BF)
        t = mm(gj, coef[j]) + lax.dot_general(
            gj, pick, (((1,), (1,)), ((), ())), preferred_element_type=F32
        )
        t_ref[:, j * size : (j + 1) * size] = t.astype(BF)
    copy.wait()
    out_ref[...] = mm(t_ref[...], block[...]).astype(BF)


def first_part(z, charges, leaf_coef, leaf_rows, local_interp):
    skel = leaf_coef.shape[1]
    rows_here, cols = charges.shape
    width = cols // len(ORDER)
    vm = pl.BlockSpec(memory_space=pltpu.VMEM)
    spec = pltpu.PrefetchScalarGridSpec(
        num_scalar_prefetch=1,
        grid=(1,),
        in_specs=[
            pl.BlockSpec((1, skel, skel), lambda i, z: (14, 0, z[0] % 8 // 4)),
            pl.BlockSpec((1, skel, skel), lambda i, z: (12 + z[0] % 8 // 4, 0, z[0] // 2 % 2)),
            pl.BlockSpec((1, skel, skel), lambda i, z: (8 + z[0] % 8 // 2, 0, z[0] % 2)),
            pl.BlockSpec((1, skel, 2 * skel), lambda i, z: (z[0] % 8, 0, 0)),
            pl.BlockSpec(leaf_coef.shape, lambda i, z: (0, 0, 0)),
            pl.BlockSpec(leaf_rows.shape, lambda i, z: (0, 0)),
            pl.BlockSpec(memory_space=pl.ANY),
        ],
        out_specs=[vm, vm],
        scratch_shapes=[pltpu.VMEM((rows_here, width), BF), pltpu.SemaphoreType.DMA],
    )
    return pl.pallas_call(
        first_kernel,
        grid_spec=spec,
        out_shape=[pltpu.VMEM((skel, rows_here), BF), pltpu.VMEM((skel, width), BF)],
        compiler_params=pltpu.CompilerParams(vmem_limit_bytes=12 << 20),
        name="first_part",
    )(z, *[hbm(local_interp)] * 4, hbm(leaf_coef), hbm(leaf_rows), hbm(charges))


def blocks_kernel(rels, z_ref, t, charges, *outs):
    width = outs[0].shape[1]
    for rel, out in zip(rels, outs):
        at = column(z_ref[0], rel, width)
        out[...] = mm(t[...], charges[:, pl.ds(at, width)]).astype(BF)


def block_parts(z, t, charges, rels):
    width = charges.shape[1] // len(ORDER)
    vm = pl.BlockSpec(memory_space=pltpu.VMEM)
    return pl.pallas_call(
        functools.partial(blocks_kernel, rels),
        in_specs=[pl.BlockSpec(memory_space=pltpu.SMEM), vm, vm],
        out_specs=[vm] * len(rels),
        out_shape=[pltpu.VMEM((t.shape[0], width), BF) for _ in rels],
        compiler_params=pltpu.CompilerParams(vmem_limit_bytes=8 << 20),
        name="blocks",
    )(z, vmem(t), vmem(charges))


def ring_sum(s, m):
    half = s[0].shape[0] // 2
    p = shift(s[4][:half], 1)
    n = shift(s[4][half:], -1)
    m = paced(m, s[4])
    x2 = swap(m[240:248], 16)
    x1 = swap(m[224:248], 8)
    x3 = swap(m[240:248], 24)

    up = jnp.concatenate([add(s[3][:half], p), s[3][half:]], 0)
    down = jnp.concatenate([s[5][:half], add(s[5][half:], n)], 0)
    p = shift(up, 1)
    n = shift(down, -1)
    x1, x2, x3, _, _ = lax.optimization_barrier((x1, x2, x3, up, down))
    v = jnp.concatenate([m[0:240], x1[0:16], m[240:248], x1[16:24], x2, x3], 0)
    y1 = swap(v[128:288], 2)
    up, down = add(s[2], p), add(s[6], n)
    p = shift(up, 1)
    n = shift(down, -1)
    y1 = paced(y1, up, down)
    y2 = swap(jnp.concatenate([v[192:288], y1[64:160]], 0), 4)
    up, down = add(s[1], p), add(s[7], n)
    p = shift(up, 1)
    n = shift(down, -1)
    w = jnp.concatenate([v, y1, paced(y2, up, down)], 0)
    wp = swap(w, 1)
    return (s[0].astype(F32) + p.astype(F32) + n.astype(F32)).astype(BF), w, wp


def compose_kernel(pos, w, wp, q_ref, p1_ref, pn):
    x, y, c = pos[0] // 8, pos[0] // 2 % 4, pos[0] % 2
    both = ((w, c), (wp, 1 - c))
    base = (128, 288, 448 - 64, 544 - 64)

    def half(ref, at, count, h):
        return ref[at : at + count, pl.ds(pl.multiple_of(h * 256, 256), 256)]

    def put(at, size, value):
        pn[pl.ds(pl.multiple_of(at * size, size), size), :] = value

    for ref, core in both:
        at = pl.ds(pl.multiple_of(core * 128, 128), 128)
        p1_ref[at, 0:256] = half(ref, 0, 128, c)
        p1_ref[at, 256:512] = half(ref, 0, 128, 1 - c)
    h2, h3, h4, h5 = y % 2, y // 2, x % 2, x // 2
    for ref, core in both:
        for ky in (0, 1):
            put((y ^ ky) % 2 * 2 + core, 64, half(ref, base[ky], 64, h2))
    q2 = pn[...]
    for ref, core in both:
        for ky in range(4):
            put((y ^ ky) * 2 + core, 32, half(ref, base[ky] + 64, 32, h3))
    q3 = mm(pn[...], q2).astype(BF)
    for ref, core in both:
        for ky in range(4):
            for kx in (0, 1):
                put((x ^ kx) % 2 * 8 + (y ^ ky) * 2 + core, 16, half(ref, base[ky] + 96 + 16 * kx, 16, h4))
    q4 = mm(pn[...], q3).astype(BF)

    r3 = [mm(half(w, base[ky] + 64, 32, h3), q2) for ky in range(4)]
    r4 = [mm(half(w, base[ky] + 96, 32, h4), q3) for ky in range(4)]
    r5 = [mm(half(w, base[ky] + 128, 32, h5), q4) for ky in range(4)]

    def level4(kx):
        return [r4[ky][16 * kx : 16 * kx + 16] for ky in range(4)]

    def level5(kx):
        return [r5[ky][8 * kx : 8 * kx + 8] for ky in range(4)]

    q_ref[0:160, :] = jnp.concatenate(level4(1) + level5(1) + level5(2) + level5(3), 0).astype(BF)
    q_ref[160:224, :] = half(w, base[0], 64, h2)
    q_ref[224:288, :] = half(w, base[1], 64, h2)
    q_ref[288:512, :] = jnp.concatenate(r3 + level4(0) + level5(0), 0).astype(BF)


def compose(pos, w, wp):
    vm = pl.BlockSpec(memory_space=pltpu.VMEM)
    return pl.pallas_call(
        compose_kernel,
        in_specs=[pl.BlockSpec(memory_space=pltpu.SMEM), vm, vm],
        out_specs=[vm, vm],
        out_shape=[pltpu.VMEM((512, 256), BF), pltpu.VMEM((256, 512), BF)],
        scratch_shapes=[pltpu.VMEM((256, 256), BF)],
        compiler_params=pltpu.CompilerParams(vmem_limit_bytes=8 << 20),
        name="compose",
    )(pos, vmem(w), vmem(wp))


def upper(pos, q, p1, root):
    other = swap(root, 1)
    n1 = (mm(p1[:, :256], root) + mm(p1[:, 256:], other)).astype(BF)
    first = lax.dynamic_slice_in_dim(n1, pos % 2 * 128, 128, 0)
    y = mm(q, n1).astype(BF)
    a2 = swap(y[96:128], 16)
    a1 = swap(y[0:96], 8)
    a3 = swap(y[128:160], 24)
    l2, l3 = y[160:288], y[288:416]
    l4 = add(y[416:480], a1[0:64])
    l5 = (
        y[480:512].astype(F32) + a1[64:96].astype(F32) + a2.astype(F32) + a3.astype(F32)
    ).astype(BF)

    def rows(k):
        return [l3[32 * k : 32 * k + 32], l4[16 * k : 16 * k + 16], l5[8 * k : 8 * k + 8]]

    b2 = swap(jnp.concatenate(rows(2), 0), 4)
    b1 = swap(jnp.concatenate([l2[64:128]] + rows(1), 0), 2)
    b3 = swap(jnp.concatenate(rows(3), 0), 6)
    near = add(l2[0:64], b1[0:64])
    far = (
        jnp.concatenate(rows(0), 0).astype(F32)
        + b1[64:120].astype(F32)
        + b2.astype(F32)
        + b3.astype(F32)
    ).astype(BF)
    return jnp.concatenate([first, near, far], 0)


def local(charges, leaf_coef, leaf_rows, local_interp, top_interp):
    pos = lax.axis_index("leaf").astype(jnp.int32)
    z = (pos % 2 * lax.axis_size("rhs") + lax.axis_index("rhs").astype(jnp.int32)).reshape(1)
    s = {}
    t, s[4] = first_part(z, charges, leaf_coef, leaf_rows, local_interp)
    for rels in ((3, 5), (2, 6), (1, 7, 0)):
        for rel, part in zip(rels, block_parts(z, t, charges, rels)):
            s[rel] = part
    root, w, wp = ring_sum(s, top_interp)
    q, p1 = compose(pos.reshape(1), w, wp)
    return root, upper(pos, q, p1, root)


def solution(mesh):
    placed = (
        P(("leaf", "rhs"), None),
        P(("leaf", "rhs"), None, None),
        P(("leaf", "rhs"), None),
        P("leaf", None, None),
        P("leaf", None),
    )

    return jax.shard_map(
        local,
        mesh=mesh,
        in_specs=placed,
        out_specs=(P("leaf", "rhs"), P("leaf", "rhs")),
        check_vma=False,
    )
```

```python
import functools

import jax
import jax.numpy as jnp
from jax import lax
from jax.experimental import pallas as pl
from jax.experimental.pallas import tpu as pltpu
from jax.sharding import PartitionSpec as P


BF = jnp.bfloat16
F32 = jnp.float32

ORDER = (4, 3, 5, 2, 6, 1, 7, 0)


def mm(a, b):
    return jnp.dot(a, b, preferred_element_type=F32)


def shift(x, distance):
    leaves, n = lax.axis_size("leaf"), lax.axis_size("rhs")
    pairs = []
    for leaf in range(leaves):
        step = distance
        pairs += [(leaf * n + i, leaf * n + (i + step) % n) for i in range(n)]
    return lax.ppermute(x, ("leaf", "rhs"), pairs)


def column(place, rel, width):
    n = len(ORDER)
    block = (place % n + rel) % n
    return pl.multiple_of(block * width, width)


def swap(x, bits):
    n = lax.axis_size("leaf")
    return lax.ppermute(x, "leaf", [(i, i ^ bits) for i in range(n)])


def vmem(x):
    return pltpu.with_memory_space_constraint(x, pltpu.VMEM)


def hbm(x):
    return pltpu.with_memory_space_constraint(x, pltpu.HBM)


def paced(x, *after):
    return lax.optimization_barrier((x, *after))[0]


def add(a, b):
    return (a.astype(F32) + b.astype(F32)).astype(BF)


def add3(a, b, c):
    return (a.astype(F32) + b.astype(F32) + c.astype(F32)).astype(BF)


def first_kernel(z_ref, l4, l3, l2, l1, coef, rows, charges, t_ref, out_ref, block, sem):
    width = block.shape[1]
    at = column(z_ref[0], ORDER[0], width)
    copy = pltpu.make_async_copy(charges.at[:, pl.ds(at, width)], block, sem)
    copy.start()
    a = mm(l4[0], l3[0]).astype(BF)
    a = mm(a, l2[0]).astype(BF)
    g = mm(a, l1[0]).astype(BF)
    skel = l1.shape[1]
    size = coef.shape[2]
    for j in range(coef.shape[0]):
        gj = g[:, j * skel : (j + 1) * skel]
        where = lax.broadcasted_iota(jnp.int32, (size, skel), 0)
        pick = jnp.where(where == rows[j : j + 1, :], 1.0, 0.0).astype(BF)
        t = mm(gj, coef[j]) + lax.dot_general(
            gj, pick, (((1,), (1,)), ((), ())), preferred_element_type=F32
        )
        t_ref[:, j * size : (j + 1) * size] = t.astype(BF)
    copy.wait()
    out_ref[...] = mm(t_ref[...], block[...]).astype(BF)


def first_part(z, charges, leaf_coef, leaf_rows, local_interp):
    skel = leaf_coef.shape[1]
    rows_here, cols = charges.shape
    width = cols // len(ORDER)
    vm = pl.BlockSpec(memory_space=pltpu.VMEM)
    spec = pltpu.PrefetchScalarGridSpec(
        num_scalar_prefetch=1,
        grid=(1,),
        in_specs=[
            pl.BlockSpec((1, skel, skel), lambda i, z: (14, 0, z[0] % 8 // 4)),
            pl.BlockSpec((1, skel, skel), lambda i, z: (12 + z[0] % 8 // 4, 0, z[0] // 2 % 2)),
            pl.BlockSpec((1, skel, skel), lambda i, z: (8 + z[0] % 8 // 2, 0, z[0] % 2)),
            pl.BlockSpec((1, skel, 2 * skel), lambda i, z: (z[0] % 8, 0, 0)),
            pl.BlockSpec(leaf_coef.shape, lambda i, z: (0, 0, 0)),
            pl.BlockSpec(leaf_rows.shape, lambda i, z: (0, 0)),
            pl.BlockSpec(memory_space=pl.ANY),
        ],
        out_specs=[vm, vm],
        scratch_shapes=[pltpu.VMEM((rows_here, width), BF), pltpu.SemaphoreType.DMA],
    )
    return pl.pallas_call(
        first_kernel,
        grid_spec=spec,
        out_shape=[pltpu.VMEM((skel, rows_here), BF), pltpu.VMEM((skel, width), BF)],
        compiler_params=pltpu.CompilerParams(vmem_limit_bytes=12 << 20),
        name="first_part",
    )(z, *[hbm(local_interp)] * 4, hbm(leaf_coef), hbm(leaf_rows), hbm(charges))


def blocks_kernel(rels, z_ref, t, charges, *outs):
    width = outs[0].shape[1]
    for rel, out in zip(rels, outs):
        at = column(z_ref[0], rel, width)
        out[...] = mm(t[...], charges[:, pl.ds(at, width)]).astype(BF)


def block_parts(z, t, charges, rels):
    width = charges.shape[1] // len(ORDER)
    vm = pl.BlockSpec(memory_space=pltpu.VMEM)
    return pl.pallas_call(
        functools.partial(blocks_kernel, rels),
        in_specs=[pl.BlockSpec(memory_space=pltpu.SMEM), vm, vm],
        out_specs=[vm] * len(rels),
        out_shape=[pltpu.VMEM((t.shape[0], width), BF) for _ in rels],
        compiler_params=pltpu.CompilerParams(vmem_limit_bytes=8 << 20),
        name="blocks",
    )(z, vmem(t), vmem(charges))


def ring_sum(s, m):
    half = s[0].shape[0] // 2
    p = shift(s[4][:half], 1)
    n = shift(s[4][half:], -1)
    m = paced(m, s[4])
    x1 = swap(m[224:248], 8)
    x2 = swap(m[240:248], 16)
    x3 = swap(m[240:248], 24)

    up = jnp.concatenate([add(s[3][:half], p), s[3][half:]], 0)
    down = jnp.concatenate([s[5][:half], add(s[5][half:], n)], 0)
    p = shift(up, 1)
    n = shift(down, -1)
    up, down = add(s[2], p), add(s[6], n)
    p = shift(up, 1)
    n = shift(down, -1)
    x1, x2, x3, _, _ = lax.optimization_barrier((x1, x2, x3, up, down))
    v = jnp.concatenate([m[0:240], x1[0:16], m[240:248], x1[16:24], x2, x3], 0)
    y2 = swap(v[192:288], 4)
    y1 = swap(v[128:288], 2)
    y3 = swap(v[192:288], 6)
    up, down = add(s[1], p), add(s[7], n)
    p = shift(up, 1)
    n = shift(down, -1)
    y1, y2, y3, _, _ = lax.optimization_barrier((y1, y2, y3, up, down))
    w = jnp.concatenate([v, y1, y2, y3], 0)
    wp = swap(w, 1)
    return add3(s[0], p, n), w, wp


def compose_kernel(pos, w, wp, q_ref, p1_ref, pn):
    x, y, c = pos[0] // 8, pos[0] // 2 % 4, pos[0] % 2
    both = ((w, c), (wp, 1 - c))
    base = (128, 288, 448 - 64, 544 - 64)

    def half(ref, at, count, h):
        return ref[at : at + count, pl.ds(pl.multiple_of(h * 256, 256), 256)]

    def put(at, size, value):
        pn[pl.ds(pl.multiple_of(at * size, size), size), :] = value

    for ref, core in both:
        at = pl.ds(pl.multiple_of(core * 128, 128), 128)
        p1_ref[at, 0:256] = half(ref, 0, 128, c)
        p1_ref[at, 256:512] = half(ref, 0, 128, 1 - c)
    h2, h3, h4, h5 = y % 2, y // 2, x % 2, x // 2
    for ref, core in both:
        for ky in (0, 1):
            put((y ^ ky) % 2 * 2 + core, 64, half(ref, base[ky], 64, h2))
    q2 = pn[...]
    for ref, core in both:
        for ky in range(4):
            put((y ^ ky) * 2 + core, 32, half(ref, base[ky] + 64, 32, h3))
    q3 = mm(pn[...], q2).astype(BF)
    for ref, core in both:
        for ky in range(4):
            for kx in (0, 1):
                put((x ^ kx) % 2 * 8 + (y ^ ky) * 2 + core, 16, half(ref, base[ky] + 96 + 16 * kx, 16, h4))
    q4 = mm(pn[...], q3).astype(BF)

    r3 = [mm(half(w, base[ky] + 64, 32, h3), q2) for ky in range(4)]
    r4 = [mm(half(w, base[ky] + 96, 32, h4), q3) for ky in range(4)]
    r5 = [mm(half(w, base[ky] + 128, 32, h5), q4) for ky in range(4)]

    def level4(kx):
        return [r4[ky][16 * kx : 16 * kx + 16] for ky in range(4)]

    def level5(kx):
        return [r5[ky][8 * kx : 8 * kx + 8] for ky in range(4)]

    q_ref[0:160, :] = jnp.concatenate(level4(1) + level5(1) + level5(2) + level5(3), 0).astype(BF)
    q_ref[160:224, :] = half(w, base[0], 64, h2)
    q_ref[224:288, :] = half(w, base[1], 64, h2)
    q_ref[288:512, :] = jnp.concatenate(r3 + level4(0) + level5(0), 0).astype(BF)


def compose(pos, w, wp):
    vm = pl.BlockSpec(memory_space=pltpu.VMEM)
    return pl.pallas_call(
        compose_kernel,
        in_specs=[pl.BlockSpec(memory_space=pltpu.SMEM), vm, vm],
        out_specs=[vm, vm],
        out_shape=[pltpu.VMEM((512, 256), BF), pltpu.VMEM((256, 512), BF)],
        scratch_shapes=[pltpu.VMEM((256, 256), BF)],
        compiler_params=pltpu.CompilerParams(vmem_limit_bytes=8 << 20),
        name="compose",
    )(pos, vmem(w), vmem(wp))


def upper(pos, q, p1, root):
    other = swap(root, 1)
    mine = lax.optimization_barrier(mm(p1[:, :256], root))
    n1 = (mine + mm(p1[:, 256:], other)).astype(BF)
    first = lax.dynamic_slice_in_dim(n1, pos % 2 * 128, 128, 0)
    y = mm(q, n1).astype(BF)
    a2 = swap(y[96:128], 16)
    a1 = swap(y[0:96], 8)
    a3 = swap(y[128:160], 24)
    l2, l3 = y[160:288], y[288:416]
    l4 = add(y[416:480], a1[0:64])
    l5 = (
        y[480:512].astype(F32) + a1[64:96].astype(F32) + a2.astype(F32) + a3.astype(F32)
    ).astype(BF)

    def rows(k):
        return [l3[32 * k : 32 * k + 32], l4[16 * k : 16 * k + 16], l5[8 * k : 8 * k + 8]]

    b2 = swap(jnp.concatenate(rows(2), 0), 4)
    b1 = swap(jnp.concatenate([l2[64:128]] + rows(1), 0), 2)
    b3 = swap(jnp.concatenate(rows(3), 0), 6)
    near = add(l2[0:64], b1[0:64])
    far = (
        jnp.concatenate(rows(0), 0).astype(F32)
        + b1[64:120].astype(F32)
        + b2.astype(F32)
        + b3.astype(F32)
    ).astype(BF)
    return jnp.concatenate([first, near, far], 0)


def local(charges, leaf_coef, leaf_rows, local_interp, top_interp):
    pos = lax.axis_index("leaf").astype(jnp.int32)
    z = (pos % 2 * lax.axis_size("rhs") + lax.axis_index("rhs").astype(jnp.int32)).reshape(1)
    s = {}
    t, s[4] = first_part(z, charges, leaf_coef, leaf_rows, local_interp)
    for rels in ((3, 5), (2, 6), (1, 7, 0)):
        for rel, part in zip(rels, block_parts(z, t, charges, rels)):
            s[rel] = part
    root, w, wp = ring_sum(s, top_interp)
    q, p1 = compose(pos.reshape(1), w, wp)
    return root, upper(pos, q, p1, root)


def solution(mesh):
    placed = (
        P(("leaf", "rhs"), None),
        P(("leaf", "rhs"), None, None),
        P(("leaf", "rhs"), None),
        P("leaf", None, None),
        P("leaf", None),
    )

    return jax.shard_map(
        local,
        mesh=mesh,
        in_specs=placed,
        out_specs=(P("leaf", "rhs"), P("leaf", "rhs")),
        check_vma=False,
    )
```

```python
import functools

import jax
import jax.numpy as jnp
from jax import lax
from jax.experimental import pallas as pl
from jax.experimental.pallas import tpu as pltpu
from jax.sharding import PartitionSpec as P


BF = jnp.bfloat16
F32 = jnp.float32

ORDER = (4, 3, 5, 2, 6, 1, 7, 0)


def mm(a, b):
    return jnp.dot(a, b, preferred_element_type=F32)


def shift(x, distance):
    n = lax.axis_size("rhs")
    pairs = [(i, (i + (-distance if i % 2 else distance)) % n) for i in range(n)]
    return lax.ppermute(x, "rhs", pairs)


def column(place, rel, width):
    n = len(ORDER)
    block = (place + jnp.where(place % 2 == 0, rel, n - rel)) % n
    return pl.multiple_of(block * width, width)


def swap(x, bits):
    n = lax.axis_size("leaf")
    return lax.ppermute(x, "leaf", [(i, i ^ bits) for i in range(n)])


def vmem(x):
    return pltpu.with_memory_space_constraint(x, pltpu.VMEM)


def hbm(x):
    return pltpu.with_memory_space_constraint(x, pltpu.HBM)


def paced(x, *after):
    return lax.optimization_barrier((x, *after))[0]


def add(a, b):
    return (a.astype(F32) + b.astype(F32)).astype(BF)


def add3(a, b, c):
    return (a.astype(F32) + b.astype(F32) + c.astype(F32)).astype(BF)


def first_kernel(z_ref, l4, l3, l2, l1, coef, rows, charges, t_ref, out_ref, block, sem):
    width = block.shape[1]
    at = column(z_ref[0], ORDER[0], width)
    copy = pltpu.make_async_copy(charges.at[:, pl.ds(at, width)], block, sem)
    copy.start()
    a = mm(l4[0], l3[0]).astype(BF)
    a = mm(a, l2[0]).astype(BF)
    g = mm(a, l1[0]).astype(BF)
    skel = l1.shape[1]
    size = coef.shape[2]
    for j in range(coef.shape[0]):
        gj = g[:, j * skel : (j + 1) * skel]
        where = lax.broadcasted_iota(jnp.int32, (size, skel), 0)
        pick = jnp.where(where == rows[j : j + 1, :], 1.0, 0.0).astype(BF)
        t = mm(gj, coef[j]) + lax.dot_general(
            gj, pick, (((1,), (1,)), ((), ())), preferred_element_type=F32
        )
        t_ref[:, j * size : (j + 1) * size] = t.astype(BF)
    copy.wait()
    out_ref[...] = mm(t_ref[...], block[...]).astype(BF)


def first_part(z, charges, leaf_coef, leaf_rows, local_interp):
    skel = leaf_coef.shape[1]
    rows_here, cols = charges.shape
    width = cols // len(ORDER)
    vm = pl.BlockSpec(memory_space=pltpu.VMEM)
    spec = pltpu.PrefetchScalarGridSpec(
        num_scalar_prefetch=1,
        grid=(1,),
        in_specs=[
            pl.BlockSpec((1, skel, skel), lambda i, z: (14, 0, z[0] // 4)),
            pl.BlockSpec((1, skel, skel), lambda i, z: (12 + z[0] // 4, 0, z[0] // 2 % 2)),
            pl.BlockSpec((1, skel, skel), lambda i, z: (8 + z[0] // 2, 0, z[0] % 2)),
            pl.BlockSpec((1, skel, 2 * skel), lambda i, z: (z[0], 0, 0)),
            pl.BlockSpec(leaf_coef.shape, lambda i, z: (0, 0, 0)),
            pl.BlockSpec(leaf_rows.shape, lambda i, z: (0, 0)),
            pl.BlockSpec(memory_space=pl.ANY),
        ],
        out_specs=[vm, vm],
        scratch_shapes=[pltpu.VMEM((rows_here, width), BF), pltpu.SemaphoreType.DMA],
    )
    return pl.pallas_call(
        first_kernel,
        grid_spec=spec,
        out_shape=[pltpu.VMEM((skel, rows_here), BF), pltpu.VMEM((skel, width), BF)],
        compiler_params=pltpu.CompilerParams(vmem_limit_bytes=12 << 20),
        name="first_part",
    )(z, *[hbm(local_interp)] * 4, hbm(leaf_coef), hbm(leaf_rows), hbm(charges))


def blocks_kernel(rels, z_ref, t, charges, *outs):
    width = outs[0].shape[1]
    for rel, out in zip(rels, outs):
        at = column(z_ref[0], rel, width)
        out[...] = mm(t[...], charges[:, pl.ds(at, width)]).astype(BF)


def block_parts(z, t, charges, rels):
    width = charges.shape[1] // len(ORDER)
    vm = pl.BlockSpec(memory_space=pltpu.VMEM)
    return pl.pallas_call(
        functools.partial(blocks_kernel, rels),
        in_specs=[pl.BlockSpec(memory_space=pltpu.SMEM), vm, vm],
        out_specs=[vm] * len(rels),
        out_shape=[pltpu.VMEM((t.shape[0], width), BF) for _ in rels],
        compiler_params=pltpu.CompilerParams(vmem_limit_bytes=8 << 20),
        name="blocks",
    )(z, vmem(t), vmem(charges))


def ring_sum(s, m):
    half = s[0].shape[0] // 2
    behind = shift(s[4][:half], 1)
    ahead = shift(s[4][half:], -1)
    m = paced(m, s[4])
    x1 = swap(m[224:248], 8)
    x2 = swap(m[240:248], 16)
    x3 = swap(m[240:248], 24)

    one = jnp.concatenate([s[3][:half], add(s[3][half:], ahead)], 0)
    two = jnp.concatenate([add(s[5][:half], behind), s[5][half:]], 0)
    behind = shift(one, 1)
    ahead = shift(two, -1)
    one, two = add(s[2], ahead), add(s[6], behind)
    behind = shift(one, 1)
    ahead = shift(two, -1)
    x1, x2, x3, _, _ = lax.optimization_barrier((x1, x2, x3, one, two))
    v = jnp.concatenate([m[0:240], x1[0:16], m[240:248], x1[16:24], x2, x3], 0)
    y2 = swap(v[192:288], 4)
    y1 = swap(v[128:288], 2)
    y3 = swap(v[192:288], 6)
    one, two = add(s[1], ahead), add(s[7], behind)
    behind = shift(one, 1)
    ahead = shift(two, -1)
    y1, y2, y3, _, _ = lax.optimization_barrier((y1, y2, y3, one, two))
    w = jnp.concatenate([v, y1, y2, y3], 0)
    wp = swap(w, 1)
    return add3(s[0], behind, ahead), w, wp


def compose_kernel(pos, w, wp, q_ref, p1_ref, pn):
    x, y, c = pos[0] // 8, pos[0] // 2 % 4, pos[0] % 2
    both = ((w, c), (wp, 1 - c))
    base = (128, 288, 448 - 64, 544 - 64)

    def half(ref, at, count, h):
        return ref[at : at + count, pl.ds(pl.multiple_of(h * 256, 256), 256)]

    def put(at, size, value):
        pn[pl.ds(pl.multiple_of(at * size, size), size), :] = value

    for ref, core in both:
        at = pl.ds(pl.multiple_of(core * 128, 128), 128)
        p1_ref[at, 0:256] = half(ref, 0, 128, c)
        p1_ref[at, 256:512] = half(ref, 0, 128, 1 - c)
    h2, h3, h4, h5 = y % 2, y // 2, x % 2, x // 2
    for ref, core in both:
        for ky in (0, 1):
            put((y ^ ky) % 2 * 2 + core, 64, half(ref, base[ky], 64, h2))
    q2 = pn[...]
    for ref, core in both:
        for ky in range(4):
            put((y ^ ky) * 2 + core, 32, half(ref, base[ky] + 64, 32, h3))
    q3 = mm(pn[...], q2).astype(BF)
    for ref, core in both:
        for ky in range(4):
            for kx in (0, 1):
                put((x ^ kx) % 2 * 8 + (y ^ ky) * 2 + core, 16, half(ref, base[ky] + 96 + 16 * kx, 16, h4))
    q4 = mm(pn[...], q3).astype(BF)

    r3 = [mm(half(w, base[ky] + 64, 32, h3), q2) for ky in range(4)]
    r4 = [mm(half(w, base[ky] + 96, 32, h4), q3) for ky in range(4)]
    r5 = [mm(half(w, base[ky] + 128, 32, h5), q4) for ky in range(4)]

    def level4(kx):
        return [r4[ky][16 * kx : 16 * kx + 16] for ky in range(4)]

    def level5(kx):
        return [r5[ky][8 * kx : 8 * kx + 8] for ky in range(4)]

    q_ref[0:160, :] = jnp.concatenate(level4(1) + level5(1) + level5(2) + level5(3), 0).astype(BF)
    q_ref[160:224, :] = half(w, base[0], 64, h2)
    q_ref[224:288, :] = half(w, base[1], 64, h2)
    q_ref[288:512, :] = jnp.concatenate(r3 + level4(0) + level5(0), 0).astype(BF)


def compose(pos, w, wp):
    vm = pl.BlockSpec(memory_space=pltpu.VMEM)
    return pl.pallas_call(
        compose_kernel,
        in_specs=[pl.BlockSpec(memory_space=pltpu.SMEM), vm, vm],
        out_specs=[vm, vm],
        out_shape=[pltpu.VMEM((512, 256), BF), pltpu.VMEM((256, 512), BF)],
        scratch_shapes=[pltpu.VMEM((256, 256), BF)],
        compiler_params=pltpu.CompilerParams(vmem_limit_bytes=8 << 20),
        name="compose",
    )(pos, vmem(w), vmem(wp))


def upper(pos, q, p1, root):
    other = swap(root, 1)
    mine = lax.optimization_barrier(mm(p1[:, :256], root))
    n1 = (mine + mm(p1[:, 256:], other)).astype(BF)
    first = lax.dynamic_slice_in_dim(n1, pos % 2 * 128, 128, 0)
    y = mm(q, n1).astype(BF)
    a2 = swap(y[96:128], 16)
    a1 = swap(y[0:96], 8)
    a3 = swap(y[128:160], 24)
    l2, l3 = y[160:288], y[288:416]
    l4 = add(y[416:480], a1[0:64])
    l5 = (
        y[480:512].astype(F32) + a1[64:96].astype(F32) + a2.astype(F32) + a3.astype(F32)
    ).astype(BF)

    def rows(k):
        return [l3[32 * k : 32 * k + 32], l4[16 * k : 16 * k + 16], l5[8 * k : 8 * k + 8]]

    b2 = swap(jnp.concatenate(rows(2), 0), 4)
    b1 = swap(jnp.concatenate([l2[64:128]] + rows(1), 0), 2)
    b3 = swap(jnp.concatenate(rows(3), 0), 6)
    near = add(l2[0:64], b1[0:64])
    far = (
        jnp.concatenate(rows(0), 0).astype(F32)
        + b1[64:120].astype(F32)
        + b2.astype(F32)
        + b3.astype(F32)
    ).astype(BF)
    return jnp.concatenate([first, near, far], 0)


def local(charges, leaf_coef, leaf_rows, local_interp, top_interp):
    pos = lax.axis_index("leaf").astype(jnp.int32)
    z = lax.axis_index("rhs").astype(jnp.int32).reshape(1)
    s = {}
    t, s[4] = first_part(z, charges, leaf_coef, leaf_rows, local_interp)
    for rels in ((3, 5), (2, 6), (1, 7, 0)):
        for rel, part in zip(rels, block_parts(z, t, charges, rels)):
            s[rel] = part
    root, w, wp = ring_sum(s, top_interp)
    q, p1 = compose(pos.reshape(1), w, wp)
    return root, upper(pos, q, p1, root)


def solution(mesh):
    placed = (
        P(("leaf", "rhs"), None),
        P(("leaf", "rhs"), None, None),
        P(("leaf", "rhs"), None),
        P("leaf", None, None),
        P("leaf", None),
    )

    return jax.shard_map(
        local,
        mesh=mesh,
        in_specs=placed,
        out_specs=(P("leaf", "rhs"), P("leaf", "rhs")),
        check_vma=False,
    )
```
